256 devices in a mesh: dev: 256 (over x, y, z, core).
Axes of the slice: x: 4, y: 4, z: 8, core: 2. Of those that a mesh axis runs over, the one named last changes fastest.
Arguments:
- diagonal: float32 [131072, 512], P('dev'), may hold values from -50 to 250, as said below
- panel: bfloat16 [786432, 512], P('dev'), may hold values from -3 to 3
- counts: int32 [256], P('dev'), may hold values from 1 to 6, 896 in all
- target_map: int32 [256, 21], P('dev'), may hold values from 0 to 7
- trailing: float32 [131072, 512], P('dev'), may hold values from -6 to 6
Outputs:
- diag_factor: float32 [131072, 512], P('dev')
- panel_factor: bfloat16 [786432, 512], P('dev')
- updated: float32 [131072, 512], P('dev')
- logdet_mean: float32 [], replicated
The draws below stay inside these ranges and needn't reach their ends.
Inputs may be any that keep to these rules, and one draw needn't show every extreme that they name: Each block of 512 rows of diagonal is symmetric positive definite. `counts`: some supernode holds 6 panel blocks.
All inputs are finite; a program needn't handle non-finite values.
Results may differ from the reference program's by a relative error of at most 0.006.
Values may be sent and summed in bfloat16 or wider, within the bound.
No kernel may reach another device: no remote copies, remote signals or barrier semaphores. Data moves between devices by JAX's collectives and lax.ppermute only.
A program may use at most 128 MiB of HBM per device.

```python
import math
import jax
import jax.numpy as jnp
import numpy as np
from jax import lax

W = 512
PB = 6
GROUP = 8
SUP = 256
PAIRS = 21
N_DEV = 256


def draw_diagonal(key, part):
    first, second = jax.random.split(jax.random.fold_in(key, 7))
    noise = jax.random.normal(first, (N_DEV, W, W), jnp.float32)
    gram = jnp.einsum('sik,sjk->sij', noise, noise) / W
    spread = jax.random.uniform(second, (N_DEV,), jnp.float32, 0.8, 1.25)
    level = jnp.exp(0.5 + 3.0 * jnp.arange(N_DEV, dtype=jnp.float32) / (N_DEV - 1))
    blocks = (level * spread)[:, None, None] * (gram + 2.0 * jnp.eye(W, dtype=jnp.float32)[None])
    return blocks.reshape(N_DEV * W, W)


def set_ends(result, own_key, smallest, top_value):
    place = [jax.random.randint(jax.random.fold_in(own_key, axis), (), 0, length) for axis, length in enumerate(result.shape)]
    main_axis = result.shape.index(max(result.shape))
    neighbour = place[:main_axis] + [(place[main_axis] + 1) % result.shape[main_axis]] + place[main_axis + 1:]
    return result.at[tuple(place)].set(smallest).at[tuple(neighbour)].set(top_value)


def levels(own_key, shape, cuts, smallest, largest):
    factor_of = 1.0
    for dim, blocks in cuts:
        steps = jax.random.uniform(jax.random.fold_in(jax.random.fold_in(own_key, 6), dim), (blocks,), jnp.float32, smallest / len(cuts), largest / len(cuts))
        factor_of = factor_of * jnp.repeat(jnp.exp(steps), shape[dim] // blocks).reshape((-1,) + (1,) * (len(shape) - 1 - dim))
    return factor_of


def split_up(amount, total, reach, skew):
    loads = [(1 << 20) // math.isqrt(standing ** skew) + 1 for standing in range(2, amount + 1)]
    surplus, given = total - reach - (amount - 1), [1] * (amount - 1)
    while surplus > 0:
        candidates = [i for i in range(amount - 1) if given[i] < reach]
        mass, left = sum([loads[i] for i in candidates]), surplus
        for i in candidates:
            extra = min(reach - given[i], max(1, left * loads[i] // mass), surplus)
            given[i] = given[i] + extra
            surplus = surplus - extra
    return np.array([reach] + given)


def ragged_sizes(key, count, total, bound, skew):
    if count == 2:
        one = jax.random.randint(key, (), max(1, total - bound), min(bound, total - 1) + 1)
        return jnp.stack([one, total - one])
    tallies = jnp.asarray(split_up(count, total, bound, skew), jnp.int32)
    twos = (count - 1) // 2
    donor, sink = tallies[1:1 + 2 * twos:2], tallies[2:2 + 2 * twos:2]
    slack = jnp.minimum(donor - 1, bound - sink)
    shifted = jax.random.randint(jax.random.fold_in(key, 1), (twos,), 0, 1 << 20) % (slack + 1)
    tallies = tallies.at[1:1 + 2 * twos:2].set(donor - shifted).at[2:2 + 2 * twos:2].set(sink + shifted)
    return tallies[jax.random.permutation(jax.random.fold_in(key, 2), count)]


def gaussian(key, dims, scale, bound, cuts=(), kind=jnp.bfloat16):
    entries = scale * jax.random.normal(key, dims, jnp.float32)
    if cuts:
        entries = entries * levels(key, dims, cuts, -0.22, 0.18)
    return jnp.clip(entries, -bound, bound).astype(kind)


def setup_inputs(seed: int = 0) -> dict:
    keys = jax.random.split(jax.random.key(seed), 6)
    return {
        "diagonal": draw_diagonal(jax.random.fold_in(keys[5], 71), 0),
        "panel": gaussian(keys[1], (SUP * PB * W, W), 0.5, 3.0, ((0, 256),)),
        "counts": ragged_sizes(keys[2], SUP, SUP * (PB + 1) // 2, PB, 0).astype(jnp.int32),
        "target_map": set_ends(jax.random.randint(keys[3], (SUP, PAIRS), 0, GROUP), jax.random.fold_in(keys[3], 1), 0, GROUP - 1).astype(jnp.int32),
        "trailing": gaussian(keys[4], (SUP * W, W), 1.0, 6.0, ((0, 256),), jnp.float32),
    }


def pair_tables(block_count):
    pair_rows = [i for i in range(block_count) for j in range(i + 1)]
    pair_cols = [j for i in range(block_count) for j in range(i + 1)]
    return (pair_rows, pair_cols)

def factor_one(diag_block, panel_block, block_count):
    factor = jnp.linalg.cholesky(diag_block)
    solved = lax.linalg.triangular_solve(factor, panel_block.astype(jnp.float32), left_side=False, lower=True, transpose_a=True)
    block_of_row = jnp.arange(PB * W, dtype=jnp.int32) // W
    solved = jnp.where((block_of_row < block_count)[:, None], solved, jnp.zeros_like(solved)).astype(jnp.bfloat16)
    logterm = 2.0 * jnp.sum(jnp.log(jnp.diagonal(factor)))
    return (factor, solved, logterm)

def reference(diagonal, panel, counts, target_map, trailing):
    diag_blocks = diagonal.reshape(N_DEV, W, W)
    panel_blocks = panel.reshape(N_DEV, PB * W, W)
    totals = trailing.reshape(N_DEV, W, W)
    pair_rows, pair_cols = pair_tables(PB)

    def eliminate(running, inputs):
        totals, logsum = running
        node_index, diag_block, panel_block, block_count, targets = inputs
        factor, solved, logterm = factor_one(diag_block, panel_block, block_count)
        base = node_index // GROUP * GROUP
        for pair_index in range(len(pair_rows)):
            left_block = solved[pair_rows[pair_index] * W:(pair_rows[pair_index] + 1) * W]
            right_block = solved[pair_cols[pair_index] * W:(pair_cols[pair_index] + 1) * W]
            update = lax.dot_general(left_block.astype(jnp.float32), right_block.astype(jnp.float32), (((1,), (1,)), ((), ())), preferred_element_type=jnp.float32)
            target_row = (base + targets[pair_index]).astype(jnp.int32)
            totals = totals.at[target_row].add(-update)
        return ((totals, logsum + logterm), (factor, solved))
    inputs = (jnp.arange(N_DEV, dtype=jnp.int32), diag_blocks, panel_blocks, counts, target_map)
    (totals, logsum), (factors, solved) = lax.scan(eliminate, (totals, jnp.zeros((), jnp.float32)), inputs)
    return (factors.reshape(N_DEV * W, W), solved.reshape(N_DEV * PB * W, W), totals.reshape(N_DEV * W, W), logsum / (N_DEV * W))
```

```python
import jax
import jax.numpy as jnp
from jax import lax
from jax.experimental import pallas as pl
from jax.experimental.pallas import tpu as pltpu
from jax.sharding import PartitionSpec as P

GROUP = 8
LEAF = 128
TILE = 8
HIGHEST = lax.Precision.HIGHEST
CORNER = (8, 128)


def dot(a, b, a_dim, b_dim, precision=None):
    return lax.dot_general(
        a,
        b,
        (((a_dim,), (b_dim,)), ((), ())),
        precision=precision,
        preferred_element_type=jnp.float32,
    )


def row_of(x, k):
    return jnp.broadcast_to(x[k : k + 1, :], CORNER)


def column_of(x, c):
    return jnp.broadcast_to(x[:, c : c + 1], CORNER)


def factor_leaf(work, upper, inverse):
    row = lax.broadcasted_iota(jnp.int32, CORNER, 0)
    tiles = LEAF // TILE
    block, unit = work[0:TILE, 0:LEAF], work[0:TILE, LEAF:]
    for t in range(tiles):
        low = t * TILE
        last = t == tiles - 1
        columns = [column_of(block, low + c) for c in range(TILE)]
        if not last:
            next_block = work[low + TILE : low + 2 * TILE, 0:LEAF]
            next_unit = work[low + TILE : low + 2 * TILE, LEAF:]
            next_columns = [column_of(next_block, low + c) for c in range(TILE)]
        pivots = jnp.ones(CORNER, jnp.float32)
        for k in range(TILE):
            pivot = row_of(columns[k], k)
            reciprocal = 1.0 / pivot
            pivots = jnp.where(row == k, pivot, pivots)
            factor = jnp.where(row > k, columns[k], 0.0) * reciprocal
            block_row, unit_row = row_of(block, k), row_of(unit, k)
            if not last:
                next_factor = next_columns[k] * reciprocal
            for c in range(k + 1, TILE):
                entry = row_of(columns[c], k)
                columns[c] = columns[c] - factor * entry
                if not last:
                    next_columns[c] = next_columns[c] - next_factor * entry
            if k < TILE - 1:
                block = block - factor * block_row
                unit = unit - factor * unit_row
            if not last:
                next_block = next_block - next_factor * block_row
                next_unit = next_unit - next_factor * unit_row
        scale = lax.rsqrt(pivots)
        block, unit = block * scale, unit * scale
        upper[low : low + TILE, :] = block
        inverse[low : low + TILE, :] = unit
        if t < tiles - 2:
            change = dot(block, jnp.concatenate([block, unit], axis=1), 0, 0, HIGHEST)
            below = low + 2 * TILE
            work[below:, :] = work[below:, :] - change[below:, :]
        if not last:
            block, unit = next_block, next_unit


def local_kernel(
    count_ref,
    target_ref,
    order_ref,
    diagonal,
    panel,
    factor,
    panel_factor,
    sums,
    logterm,
    matrix,
    work,
    upper,
    leaf_inverse,
    inverse,
    total,
    pair_rows,
    pair_cols,
):
    width = diagonal.shape[0]
    blocks = panel.shape[0] // width
    leaves = width // LEAF
    matrix[:, 0:width] = diagonal[...]
    matrix[:, width:] = jnp.zeros((width, width), jnp.float32)
    row = lax.broadcasted_iota(jnp.int32, (LEAF, LEAF), 0)
    column = lax.broadcasted_iota(jnp.int32, (LEAF, LEAF), 1)

    def eliminate(leaf, logs):
        start = pl.multiple_of(leaf * LEAF, LEAF)
        work[:, 0:LEAF] = matrix[pl.ds(start, LEAF), pl.ds(start, LEAF)]
        work[:, LEAF:] = jnp.where(row == column, 1.0, 0.0)
        factor_leaf(work, upper, leaf_inverse)
        rows_up = upper[...]
        factor[pl.ds(start, LEAF), pl.ds(start, LEAF)] = jnp.where(row >= column, rows_up.T, 0.0)
        diagonal_row = jnp.sum(jnp.where(row == column, rows_up, 0.0), axis=0, keepdims=True)
        own_inverse = leaf_inverse[...]
        for known in range(leaves):

            @pl.when(leaf == known)
            def _():
                low, high = known * LEAF, (known + 1) * LEAF
                if known > 0:
                    inverse[low:high, 0:low] = dot(
                        own_inverse, matrix[low:high, width : width + low], 1, 0, HIGHEST
                    )
                inverse[low:high, low:high] = own_inverse
                if known < leaves - 1:
                    inverse[low:high, high:] = jnp.zeros((LEAF, width - high), jnp.float32)
                    factor[low:high, high:] = jnp.zeros((LEAF, width - high), jnp.float32)
                    below = dot(matrix[high:, low:high], own_inverse, 1, 1, HIGHEST)
                    factor[high:, low:high] = below
                    matrix[high:, high:width] = matrix[high:, high:width] - dot(
                        below, below, 1, 1, HIGHEST
                    )
                    matrix[high:, width : width + high] = matrix[
                        high:, width : width + high
                    ] - dot(below, inverse[low:high, 0:high], 1, 0, HIGHEST)

        return logs + jnp.log(diagonal_row)

    logs = lax.fori_loop(0, leaves, eliminate, jnp.zeros((1, LEAF), jnp.float32))
    logterm[...] = jnp.broadcast_to(2.0 * jnp.sum(logs), CORNER)

    count = count_ref[0]
    half = width // 2
    coarse = inverse[...].astype(jnp.bfloat16)
    fine = (inverse[...] - coarse.astype(jnp.float32)).astype(jnp.bfloat16)

    def solve(b, carry):
        rows = pl.ds(pl.multiple_of(b * width, width), width)
        entries = panel[rows, :]
        left = dot(entries[:, 0:half], coarse[0:half, 0:half], 1, 1) + dot(
            entries[:, 0:half], fine[0:half, 0:half], 1, 1
        )
        right = dot(entries, coarse[half:, :], 1, 1) + dot(entries, fine[half:, :], 1, 1)
        panel_factor[rows, 0:half] = left.astype(jnp.bfloat16)
        panel_factor[rows, half:] = right.astype(jnp.bfloat16)
        return carry

    lax.fori_loop(0, count, solve, 0)

    def clear(b, carry):
        rows = pl.ds(pl.multiple_of(b * width, width), width)
        panel_factor[rows, :] = jnp.zeros((width, width), jnp.bfloat16)
        return carry

    lax.fori_loop(count, blocks, clear, 0)

    def list_row(i, p):
        def list_pair(j, p):
            pair_rows[p] = i
            pair_cols[p] = j
            return p + 1

        return lax.fori_loop(0, i + 1, list_pair, p)

    pairs = lax.fori_loop(0, count, list_row, 0)

    def collect(slot, carry):
        target = order_ref[slot]
        total[...] = jnp.zeros((width, width), jnp.float32)

        def visit(p, carry):
            @pl.when(target_ref[p] == target)
            def _():
                left = panel_factor[pl.ds(pl.multiple_of(pair_rows[p] * width, width), width), :]
                right = panel_factor[pl.ds(pl.multiple_of(pair_cols[p] * width, width), width), :]
                total[...] = total[...] + dot(left, right, 1, 1)

            return carry

        lax.fori_loop(0, pairs, visit, 0)
        sums[slot] = total[...].astype(jnp.bfloat16)
        return carry

    lax.fori_loop(0, GROUP, collect, 0)


def work_locally(diagonal, panel, counts, targets, order):
    width = diagonal.shape[1]
    pairs = targets.shape[0]
    smem = pl.BlockSpec(memory_space=pltpu.SMEM)
    vmem = pl.BlockSpec(memory_space=pltpu.VMEM)
    return pl.pallas_call(
        local_kernel,
        in_specs=[smem, smem, smem, vmem, vmem],
        out_specs=[vmem, vmem, vmem, vmem],
        out_shape=(
            jax.ShapeDtypeStruct((width, width), jnp.float32),
            jax.ShapeDtypeStruct(panel.shape, jnp.bfloat16),
            jax.ShapeDtypeStruct((GROUP, width, width), jnp.bfloat16),
            jax.ShapeDtypeStruct(CORNER, jnp.float32),
        ),
        scratch_shapes=[
            pltpu.VMEM((width, 2 * width), jnp.float32),
            pltpu.VMEM((LEAF, 2 * LEAF), jnp.float32),
            pltpu.VMEM((LEAF, LEAF), jnp.float32),
            pltpu.VMEM((LEAF, LEAF), jnp.float32),
            pltpu.VMEM((width, width), jnp.float32),
            pltpu.VMEM((width, width), jnp.float32),
            pltpu.SMEM((pairs,), jnp.int32),
            pltpu.SMEM((pairs,), jnp.int32),
        ],
        compiler_params=pltpu.CompilerParams(vmem_limit_bytes=56 * 2**20),
        name="eliminate",
    )(counts, targets, order, diagonal, panel)


def routes(size, moves):
    return [
        (base + 2 * a + core, base + 2 * b + core)
        for base in range(0, size, GROUP)
        for core in range(2)
        for a, b in moves
    ]


def local(diagonal, panel, counts, target_map, trailing):
    width = diagonal.shape[1]
    size = lax.axis_size("dev")
    me = lax.axis_index("dev")
    core, chip = me % 2, me % GROUP // 2
    slots = jnp.arange(4, dtype=jnp.int32)
    chips = jnp.where(chip < 2, 3 - slots, slots)
    order = jnp.concatenate([2 * chips + (1 - core), 2 * chips + core]).astype(jnp.int32)
    factor, panel_factor, sums, logterm = work_locally(
        diagonal, panel, counts, target_map[0], order
    )

    def move(x, moves):
        return lax.ppermute(x, "dev", moves)

    def add(x, y):
        return (x.astype(jnp.float32) + y.astype(jnp.float32)).astype(jnp.bfloat16)

    swap = [(d, d ^ 1) for d in range(size)]
    merged = [add(sums[4 + s], move(sums[s], swap)) for s in range(4)]
    inward = routes(size, [(0, 1), (3, 2)])
    across = routes(size, [(1, 2), (2, 1)])
    outward = routes(size, [(2, 3), (1, 0)])
    first = move(merged[0], inward)
    second = move(merged[1], inward)
    third = move(merged[2], inward)
    fourth = move(add(merged[0], first), across)
    fifth = move(add(merged[1], second), across)
    sixth = move(add(merged[3], fourth), outward)
    outer = (chip == 0) | (chip == 3)
    own = jnp.where(outer, merged[3], merged[2]).astype(jnp.float32)
    updated = trailing - (
        own + third.astype(jnp.float32) + fifth.astype(jnp.float32) + sixth.astype(jnp.float32)
    )
    logsum = logterm[0:1, :]
    distance = 1
    while distance < size:
        logsum = logsum + move(logsum, [(d, d ^ distance) for d in range(size)])
        distance *= 2
    logdet_mean = logsum[0, 0] / (size * width)
    return (factor, panel_factor, updated, logdet_mean)


def solution(mesh):
    return jax.shard_map(
        local,
        mesh=mesh,
        in_specs=(P("dev", None), P("dev", None), P("dev"), P("dev", None), P("dev", None)),
        out_specs=(P("dev", None), P("dev", None), P("dev", None), P()),
        check_vma=False,
    )
```

```python
import jax
import jax.numpy as jnp
from jax import lax
from jax.experimental import pallas as pl
from jax.experimental.pallas import tpu as pltpu
from jax.sharding import PartitionSpec as P


GROUP = 8
LEAF = 128
TILE = 8
AHEAD = 3
HIGHEST = lax.Precision.HIGHEST
CORNER = (8, 128)


def dot(a, b, a_dim, b_dim, precision=None):
    return lax.dot_general(
        a,
        b,
        (((a_dim,), (b_dim,)), ((), ())),
        precision=precision,
        preferred_element_type=jnp.float32,
    )


def row_of(x, k):
    return jnp.broadcast_to(x[k : k + 1, :], CORNER)


def column_of(x, c):
    return jnp.broadcast_to(x[:, c : c + 1], CORNER)


def split(x, terms):
    parts = []
    for _ in range(terms):
        parts.append(x.astype(jnp.bfloat16))
        x = x - parts[-1].astype(jnp.float32)
    return parts


def stack(parts):
    return jnp.concatenate([x.astype(jnp.float32) for x in parts], axis=0).astype(jnp.bfloat16)


def factor_leaf(work, upper, inverse, one):
    row = lax.broadcasted_iota(jnp.int32, CORNER, 0)
    tiles = LEAF // TILE
    block = [work[t * TILE : (t + 1) * TILE, 0:LEAF] for t in range(tiles)]
    unit = [work[t * TILE : (t + 1) * TILE, LEAF:] for t in range(tiles)]
    for t in range(tiles):
        low = t * TILE
        near = range(t, min(tiles, t + 1 + AHEAD))
        far = range(t + 1 + AHEAD, tiles)
        columns = {g: [column_of(block[g], low + c) for c in range(TILE)] for g in near}
        columns[t] = [x * one for x in columns[t]]
        pivots = jnp.ones(CORNER, jnp.float32)
        for k in range(TILE):
            pivot = row_of(columns[t][k], k)
            reciprocal = 1.0 / pivot
            pivots = jnp.where(row == k, pivot, pivots)
            block_row, unit_row = row_of(block[t], k), row_of(unit[t], k)
            entries = [row_of(columns[t][c], k) for c in range(k + 1, TILE)]
            for g in near:
                if g == t and k == TILE - 1:
                    continue
                factor = columns[g][k]
                if g == t:
                    factor = jnp.where(row > k, factor, 0.0)
                factor = factor * reciprocal
                for c in range(k + 1, TILE):
                    columns[g][c] = columns[g][c] - factor * entries[c - k - 1]
                block[g] = block[g] - factor * block_row
                unit[g] = unit[g] - factor * unit_row
        scale = lax.rsqrt(pivots)
        block[t], unit[t] = block[t] * scale, unit[t] * scale
        upper[low : low + TILE, :] = block[t]
        inverse[low : low + TILE, :] = unit[t]
        if len(far):
            b, u = split(block[t], 3), split(unit[t], 3)
            pairs = [(0, 0), (0, 1), (1, 0), (0, 2), (1, 1), (2, 0)]
            left = stack([b[i] for i, _ in pairs])
            right = jnp.concatenate(
                [stack([b[j] for _, j in pairs]), stack([u[j] for _, j in pairs])], axis=1
            )
            change = dot(left, right, 0, 0)
            for g in far:
                rows = slice(g * TILE, (g + 1) * TILE)
                block[g] = block[g] - change[rows, 0:LEAF]
                unit[g] = unit[g] - change[rows, LEAF:]


def eliminate_kernel(
    count_ref,
    target_ref,
    order_ref,
    diagonal,
    panel,
    factor,
    panel_factor,
    sent,
    kept,
    logterm,
    matrix,
    work,
    upper,
    leaf_inverse,
    inverse,
    total,
    pair_rows,
    pair_cols,
):
    width = diagonal.shape[0]
    blocks = panel.shape[0] // width
    leaves = width // LEAF
    count = count_ref[0]
    one = jnp.where(jnp.full(CORNER, count, jnp.int32) > 0, 1.0, 0.0)
    matrix[:, 0:width] = diagonal[...]
    matrix[:, width:] = jnp.zeros((width, width), jnp.float32)
    row = lax.broadcasted_iota(jnp.int32, (LEAF, LEAF), 0)
    column = lax.broadcasted_iota(jnp.int32, (LEAF, LEAF), 1)

    def eliminate(leaf, logs):
        start = pl.multiple_of(leaf * LEAF, LEAF)
        work[:, 0:LEAF] = matrix[pl.ds(start, LEAF), pl.ds(start, LEAF)]
        work[:, LEAF:] = jnp.where(row == column, 1.0, 0.0)
        factor_leaf(work, upper, leaf_inverse, one)
        rows_up = upper[...]
        factor[pl.ds(start, LEAF), pl.ds(start, LEAF)] = jnp.where(row >= column, rows_up.T, 0.0)
        diagonal_row = jnp.sum(jnp.where(row == column, rows_up, 0.0), axis=0, keepdims=True)
        own_inverse = leaf_inverse[...]
        for known in range(leaves):

            @pl.when(leaf == known)
            def _():
                low, high = known * LEAF, (known + 1) * LEAF
                if known > 0:
                    inverse[low:high, 0:low] = dot(
                        own_inverse, matrix[low:high, width : width + low], 1, 0, HIGHEST
                    )
                inverse[low:high, low:high] = own_inverse
                if known < leaves - 1:
                    inverse[low:high, high:] = jnp.zeros((LEAF, width - high), jnp.float32)
                    factor[low:high, high:] = jnp.zeros((LEAF, width - high), jnp.float32)
                    below = dot(matrix[high:, low:high], own_inverse, 1, 1, HIGHEST)
                    factor[high:, low:high] = below
                    matrix[high:, high:width] = matrix[high:, high:width] - dot(
                        below, below, 1, 1, HIGHEST
                    )
                    matrix[high:, width : width + high] = matrix[
                        high:, width : width + high
                    ] - dot(below, inverse[low:high, 0:high], 1, 0, HIGHEST)

        return logs + jnp.log(diagonal_row)

    logs = lax.fori_loop(0, leaves, eliminate, jnp.zeros((1, LEAF), jnp.float32))
    logterm[...] = jnp.broadcast_to(2.0 * jnp.sum(logs), (1, LEAF))

    half = width // 2
    coarse = inverse[...].astype(jnp.bfloat16)
    fine = (inverse[...] - coarse.astype(jnp.float32)).astype(jnp.bfloat16)

    def solve(b, carry):
        rows = pl.ds(pl.multiple_of(b * width, width), width)
        entries = panel[rows, :]
        left = dot(entries[:, 0:half], coarse[0:half, 0:half], 1, 1) + dot(
            entries[:, 0:half], fine[0:half, 0:half], 1, 1
        )
        right = dot(entries, coarse[half:, :], 1, 1) + dot(entries, fine[half:, :], 1, 1)
        panel_factor[rows, 0:half] = left.astype(jnp.bfloat16)
        panel_factor[rows, half:] = right.astype(jnp.bfloat16)
        return carry

    lax.fori_loop(0, count, solve, 0)

    def clear(b, carry):
        rows = pl.ds(pl.multiple_of(b * width, width), width)
        panel_factor[rows, :] = jnp.zeros((width, width), jnp.bfloat16)
        return carry

    lax.fori_loop(count, blocks, clear, 0)
    collect(
        count, target_ref, order_ref, panel_factor, sent, kept, total, pair_rows, pair_cols
    )


def collect(count, target_ref, order_ref, panel_factor, sent, kept, total, pair_rows, pair_cols):
    width = total.shape[1]

    def list_row(i, p):
        def list_pair(j, p):
            pair_rows[p] = i
            pair_cols[p] = j
            return p + 1

        return lax.fori_loop(0, i + 1, list_pair, p)

    pairs = lax.fori_loop(0, count, list_row, 0)
    total[...] = jnp.zeros(total.shape, jnp.float32)

    def visit(p, carry):
        target = target_ref[p]

        @pl.when((target == order_ref[0]) | (target == order_ref[1]))
        def _():
            place = jnp.where(target == order_ref[0], 0, 1)
            left = panel_factor[pl.ds(pl.multiple_of(pair_rows[p] * width, width), width), :]
            right = panel_factor[pl.ds(pl.multiple_of(pair_cols[p] * width, width), width), :]
            total[place] = total[place] + dot(left, right, 1, 1)

        return carry

    lax.fori_loop(0, pairs, visit, 0)
    sent[...] = total[0].astype(jnp.bfloat16)
    kept[...] = total[1].astype(jnp.bfloat16)


def collect_kernel(
    count_ref, target_ref, order_ref, panel_factor, sent, kept, total, pair_rows, pair_cols
):
    collect(
        count_ref[0], target_ref, order_ref, panel_factor, sent, kept, total, pair_rows, pair_cols
    )


SMEM = pl.BlockSpec(memory_space=pltpu.SMEM)
VMEM = pl.BlockSpec(memory_space=pltpu.VMEM)


def eliminate(counts, targets, order, diagonal, panel):
    width = diagonal.shape[1]
    pairs = targets.shape[0]
    return pl.pallas_call(
        eliminate_kernel,
        in_specs=[SMEM, SMEM, SMEM, VMEM, VMEM],
        out_specs=[VMEM] * 5,
        out_shape=(
            jax.ShapeDtypeStruct((width, width), jnp.float32),
            jax.ShapeDtypeStruct(panel.shape, jnp.bfloat16),
            jax.ShapeDtypeStruct((width, width), jnp.bfloat16),
            jax.ShapeDtypeStruct((width, width), jnp.bfloat16),
            jax.ShapeDtypeStruct((1, LEAF), jnp.float32),
        ),
        scratch_shapes=[
            pltpu.VMEM((width, 2 * width), jnp.float32),
            pltpu.VMEM((LEAF, 2 * LEAF), jnp.float32),
            pltpu.VMEM((LEAF, LEAF), jnp.float32),
            pltpu.VMEM((LEAF, LEAF), jnp.float32),
            pltpu.VMEM((width, width), jnp.float32),
            pltpu.VMEM((2, width, width), jnp.float32),
            pltpu.SMEM((pairs,), jnp.int32),
            pltpu.SMEM((pairs,), jnp.int32),
        ],
        compiler_params=pltpu.CompilerParams(vmem_limit_bytes=40 * 2**20),
        name="eliminate",
    )(counts, targets, order, diagonal, panel)


def collect_sums(counts, targets, order, panel_factor):
    width = panel_factor.shape[1]
    pairs = targets.shape[0]
    return pl.pallas_call(
        collect_kernel,
        in_specs=[SMEM, SMEM, SMEM, VMEM],
        out_specs=[VMEM] * 2,
        out_shape=(jax.ShapeDtypeStruct((width, width), jnp.bfloat16),) * 2,
        scratch_shapes=[
            pltpu.VMEM((2, width, width), jnp.float32),
            pltpu.SMEM((pairs,), jnp.int32),
            pltpu.SMEM((pairs,), jnp.int32),
        ],
        compiler_params=pltpu.CompilerParams(vmem_limit_bytes=24 * 2**20),
        name="collect",
    )(counts, targets, order, panel_factor)


def routes(size, moves):
    return [
        (base + 2 * a + core, base + 2 * b + core)
        for base in range(0, size, GROUP)
        for core in range(2)
        for a, b in moves
    ]


def after(x, *others):
    return lax.optimization_barrier((x, *others))[0]


def local(diagonal, panel, counts, target_map, trailing):
    width = diagonal.shape[1]
    size = lax.axis_size("dev")
    me = lax.axis_index("dev")
    core, chip = me % 2, me % GROUP // 2
    targets = target_map[0]

    def order(slot):
        target_chip = jnp.where(chip < 2, 3 - slot, slot)
        return jnp.stack([2 * target_chip + 1 - core, 2 * target_chip + core]).astype(jnp.int32)

    def move(x, moves):
        return lax.ppermute(x, "dev", moves)

    def add(x, y):
        return (x.astype(jnp.float32) + y.astype(jnp.float32)).astype(jnp.bfloat16)

    def exchange(x, distance):
        return x + move(x, [(d, d ^ distance) for d in range(size)])

    def collect_for(slot_order):
        return collect_sums(counts, targets, slot_order, panel_factor)

    swap = [(d, d ^ 1) for d in range(size)]
    inward = routes(size, [(0, 1), (3, 2)])
    across = routes(size, [(1, 2), (2, 1)])
    outward = routes(size, [(2, 3), (1, 0)])

    orders = [order(slot) for slot in range(4)]
    factor, panel_factor, sent, kept, logs = eliminate(counts, targets, orders[0], diagonal, panel)
    other = move(sent, swap)
    logs = exchange(logs, 1)
    sent_b, kept_b = collect_for(orders[1])
    merged_a = add(after(kept, sent_b), other)
    first = move(merged_a, inward)
    other_b = move(sent_b, swap)
    logs = exchange(logs, 2)
    sent_c, kept_c = collect_for(after(orders[2], merged_a))
    merged_b = add(after(kept_b, sent_c), other_b)
    second = move(merged_b, inward)
    other_c = move(sent_c, swap)
    logs = exchange(logs, 4)
    sent_d, kept_d = collect_for(after(orders[3], merged_b))
    merged_c = add(after(kept_c, sent_d), other_c)
    third = move(merged_c, inward)
    other_d = move(sent_d, swap)
    logs = exchange(logs, 8)
    merged_d = add(after(kept_d, merged_c), other_d)
    outer = (chip == 0) | (chip == 3)
    base = trailing - jnp.where(outer, merged_d, merged_c).astype(jnp.float32)
    quarter = add(after(merged_a, base, merged_d), first)
    fourth = move(quarter, across)
    logs = exchange(logs, 16)
    logs = exchange(logs, 32)
    half = add(after(merged_b, quarter), second)
    fifth = move(half, across)
    logs = exchange(logs, 64)
    sixth = move(add(after(merged_d, half), fourth), outward)
    logs = exchange(logs, 128)
    updated = base - (
        third.astype(jnp.float32) + fifth.astype(jnp.float32) + sixth.astype(jnp.float32)
    )
    logdet_mean = logs[0, 0] / (size * width)
    return (factor, panel_factor, updated, logdet_mean)


def solution(mesh):
    return jax.shard_map(
        local,
        mesh=mesh,
        in_specs=(P("dev", None), P("dev", None), P("dev"), P("dev", None), P("dev", None)),
        out_specs=(P("dev", None), P("dev", None), P("dev", None), P()),
        check_vma=False,
    )
```
